32 devices in a mesh: row: 8 (over z, core), col: 2 (over x), rep: 2 (over y).
Axes of the slice: x: 2, y: 2, z: 4, core: 2. Of those that a mesh axis runs over, the one named last changes fastest.
Arguments:
- features: bfloat16 [16384, 512], P(('rep', 'col', 'row')), parts along dimension 0, may hold values from -6 to 6
- weights: bfloat16 [512, 512], replicated, may hold values from -0.25 to 0.25
- bias_vector: float32 [512], replicated, may hold values from -3 to 3
- tile_values: bfloat16 [16, 2, 128, 128, 128], P(('rep', 'row'), 'col'), parts along dimension 0, may hold values from -0.15625 to 0.15625
- tile_rows: int32 [16, 2, 128], P(('rep', 'row'), 'col'), parts along dimension 0, may hold values from 0 to 7, as said below
- tile_cols: int32 [16, 2, 128], P(('rep', 'row'), 'col'), parts along dimension 0, may hold values from 0 to 31, as said below
- tile_counts: int32 [16, 2], P(('rep', 'row'), 'col'), parts along dimension 0, may hold values from 8 to 128, as said below
- cotangent: bfloat16 [16384, 512], P(('rep', 'row', 'col')), parts along dimension 0, may hold values from -6 to 6
Outputs:
- activated: bfloat16 [16384, 512], P(('rep', 'row', 'col')), parts along dimension 0
- weight_grad: float32 [1024, 512], P('rep'), parts along dimension 0
- bias_grad: float32 [1024], P('rep'), parts along dimension 0
- feature_grad: bfloat16 [16384, 512], P(('rep', 'col', 'row')), parts along dimension 0
The draws below stay inside these ranges and needn't reach their ends.
There are 2 independent parts, one for each index of `rep`. The reference program is written for one: setup_inputs(seed, part) draws one part's arguments, and reference() takes and returns one part's arrays. A program takes and returns all parts, laid end to end along the dimension named above; an argument that names none is the same for every part. Nothing has to cross between parts.
Inputs may be any that keep to these rules, and one draw needn't show every extreme that they name: `tile_counts`: live slots of every grid cell; some cell holds exactly 128. `tile_cols`: among a cell's first tile_counts slots the column indices never fall; later slots hold arbitrary indices of the range. A (row, column) pair may repeat, and then its tiles add. `tile_rows`: slots past a cell's count hold arbitrary indices of the range.
All inputs are finite; a program needn't handle non-finite values.
Results may differ from the reference program's by a relative error of at most 0.01.
Values may be sent and summed in bfloat16 or wider, within the bound.
A program may use at most 128 MiB of HBM per device.

```python
import jax
import jax.numpy as jnp
from jax import lax

F = 512
TILE = 128
VDEV = 512
TMAX = 128
VERTICES = 8192
TROWS = 8
TCOLS = 32
N_ROW = 8
N_COL = 2


def graph_layout(key):
    base = jax.random.fold_in(key, 7)
    keys = jax.random.split(base, 5)
    cells = N_ROW * N_COL
    first = jax.random.randint(keys[0], (cells,), 1, TMAX + 1)
    second = jax.random.randint(keys[1], (cells,), 1, TMAX + 1)
    counts = jnp.maximum(first * second // TMAX, TMAX // 16)
    fullest = jax.random.randint(keys[2], (), 0, cells)
    counts = jnp.where(jnp.arange(cells) == fullest, TMAX, counts).astype(jnp.int32)
    rows_drawn = jax.random.randint(keys[3], (cells, TMAX), 0, TROWS)
    cols_drawn = jax.random.randint(keys[4], (cells, TMAX), 0, TCOLS)
    slots = jnp.arange(TMAX)[None, :]
    live = slots < counts[:, None]
    keyed = jnp.where(live, cols_drawn, cols_drawn + TCOLS)
    ordered = jnp.sort(keyed, axis=1)
    cols_out = jnp.where(ordered >= TCOLS, ordered - TCOLS, ordered)
    return (rows_drawn.reshape(N_ROW, N_COL, TMAX).astype(jnp.int32), cols_out.reshape(N_ROW, N_COL, TMAX).astype(jnp.int32), counts.reshape(N_ROW, N_COL))


def draw_tile_rows(key, part):
    return graph_layout(key)[0]


def draw_tile_cols(key, part):
    return graph_layout(key)[1]


def draw_tile_counts(key, part):
    return graph_layout(key)[2]


def steps_of(stream_key, shape, cuts, least, largest):
    def one(axis_at, blocks):
        draws = jax.random.uniform(jax.random.fold_in(jax.random.fold_in(stream_key, 6), axis_at), (blocks,), jnp.float32, least / len(cuts), largest / len(cuts))
        return jnp.repeat(jnp.exp(draws), shape[axis_at] // blocks).reshape((-1,) + (1,) * (len(shape) - axis_at - 1))

    gain = one(*cuts[0])
    for cut in cuts[1:]:
        gain = gain * one(*cut)
    return gain


def centred(stream_key, dims, scale, bound, pieces=(), held_as=jnp.bfloat16):
    array = scale * jax.random.normal(stream_key, dims, jnp.float32)
    if pieces:
        array = array * steps_of(stream_key, dims, pieces, -0.22, 0.18)
    return jnp.clip(array, -bound, bound).astype(held_as)


def setup_inputs(seed: int = 0, part: int = 0) -> dict:
    streams_of = jax.random.split(jax.random.key(seed), 9)
    part_splits = jax.random.split(jax.random.fold_in(streams_of[8], part), 9)
    features = centred(part_splits[0], (VERTICES, F), 1.0, 6.0, ((0, 16),))
    weights = centred(streams_of[1], (F, F), F ** -0.5, 0.25)
    bias_vector = centred(streams_of[2], (F,), 0.5, 3.0, (), jnp.float32)
    tile_values = centred(part_splits[3], (N_ROW, N_COL, TMAX, TILE, TILE), (TMAX * TILE * TILE // (3 * VDEV)) ** -0.5, 0.15625, ((0, 8), (1, 2)))
    tile_rows = draw_tile_rows(jax.random.fold_in(jax.random.fold_in(streams_of[8], part), 71), part)
    tile_cols = draw_tile_cols(jax.random.fold_in(jax.random.fold_in(streams_of[8], part), 71), part)
    tile_counts = draw_tile_counts(jax.random.fold_in(jax.random.fold_in(streams_of[8], part), 71), part)
    cotangent = centred(part_splits[7], (VERTICES, F), 1.0, 6.0, ((0, 16),))
    return {"features": features, "weights": weights, "bias_vector": bias_vector, "tile_values": tile_values, "tile_rows": tile_rows, "tile_cols": tile_cols, "tile_counts": tile_counts, "cotangent": cotangent}


def cell_forward(tiles, rows_in, cols_in, live_count, column_block):
    blocks = column_block.reshape(TCOLS, TILE, F)
    taken = jnp.take(blocks, cols_in, axis=0).astype(jnp.float32)
    product = jnp.einsum('tij,tjf->tif', tiles.astype(jnp.float32), taken)
    live = (jnp.arange(TMAX, dtype=jnp.int32) < live_count).astype(jnp.float32)
    product = product * live[:, None, None]
    total = jnp.zeros((TROWS, TILE, F), jnp.float32).at[rows_in].add(product)
    return total.reshape(TROWS * TILE, F)

def cell_backward(tiles, rows_in, cols_in, live_count, row_block):
    blocks = row_block.reshape(TROWS, TILE, F)
    taken = jnp.take(blocks, rows_in, axis=0).astype(jnp.float32)
    product = jnp.einsum('tji,tjf->tif', tiles.astype(jnp.float32), taken)
    live = (jnp.arange(TMAX, dtype=jnp.int32) < live_count).astype(jnp.float32)
    product = product * live[:, None, None]
    total = jnp.zeros((TCOLS, TILE, F), jnp.float32).at[cols_in].add(product)
    return total.reshape(TCOLS * TILE, F)

def reference(features, weights, bias_vector, tile_values, tile_rows, tile_cols, tile_counts, cotangent):
    column_blocks = features.reshape(N_COL, VDEV * N_ROW, F)

    def row_group(ridx):

        def over_cols(acc, cidx):
            part = cell_forward(tile_values[ridx, cidx], tile_rows[ridx, cidx], tile_cols[ridx, cidx], tile_counts[ridx, cidx], column_blocks[cidx])
            part = lax.optimization_barrier(part.astype(jnp.bfloat16))
            return (acc + part.astype(jnp.float32), None)
        acc, _ = lax.scan(over_cols, jnp.zeros((TROWS * TILE, F), jnp.float32), jnp.arange(N_COL, dtype=jnp.int32))
        return acc
    gathered = lax.map(row_group, jnp.arange(N_ROW, dtype=jnp.int32)).reshape(VERTICES, F).astype(jnp.bfloat16)
    pre = jnp.dot(gathered, weights, preferred_element_type=jnp.float32) + bias_vector
    sig = jax.nn.sigmoid(pre)
    activated = (pre * sig).astype(jnp.bfloat16)
    dpre = (cotangent.astype(jnp.float32) * sig * (1.0 + pre * (1.0 - sig))).astype(jnp.bfloat16)
    scale = 1.0 / jnp.sqrt(jnp.float32(VERTICES))
    weight_grad = lax.dot_general(gathered, dpre, (((0,), (0,)), ((), ())), preferred_element_type=jnp.float32) * scale
    bias_grad = lax.optimization_barrier(jnp.sum(dpre.astype(jnp.float32), axis=0)) * scale
    dgathered = lax.dot_general(dpre, weights, (((1,), (1,)), ((), ())), preferred_element_type=jnp.float32).astype(jnp.bfloat16)
    row_blocks = dgathered.reshape(N_ROW, VDEV * N_COL, F)

    def col_group(cidx):

        def over_rows(acc, ridx):
            part = cell_backward(tile_values[ridx, cidx], tile_rows[ridx, cidx], tile_cols[ridx, cidx], tile_counts[ridx, cidx], row_blocks[ridx])
            part = lax.optimization_barrier(part.astype(jnp.bfloat16))
            return (acc + part.astype(jnp.float32), None)
        acc, _ = lax.scan(over_rows, jnp.zeros((TCOLS * TILE, F), jnp.float32), jnp.arange(N_ROW, dtype=jnp.int32))
        return acc
    feature_grad = lax.map(col_group, jnp.arange(N_COL, dtype=jnp.int32)).reshape(VERTICES, F).astype(jnp.bfloat16)
    return (activated, weight_grad, bias_grad, feature_grad)
```

```python
import functools
import math

import jax
import jax.numpy as jnp
from jax import lax
from jax.experimental import pallas as pl
from jax.experimental.pallas import tpu as pltpu
from jax.sharding import PartitionSpec as P

slot_group = 16
feature_chunks = 2


def tile_range(cols_in, live_count, first_block, last_block):
    slots = jnp.arange(cols_in.shape[0], dtype=jnp.int32)
    live = slots < live_count
    lower = jnp.sum((live & (cols_in < first_block)).astype(jnp.int32))
    upper = jnp.sum((live & (cols_in < last_block)).astype(jnp.int32))
    return (lower, upper)


def group_slots(tiles, rows_in, cols_in, begin, upper):
    limit = tiles.shape[0] - slot_group
    start = jnp.minimum(begin, limit)
    tile_group = lax.dynamic_slice_in_dim(tiles, start, slot_group, 0)
    row_group = lax.dynamic_slice_in_dim(rows_in, start, slot_group, 0)
    col_group = lax.dynamic_slice_in_dim(cols_in, start, slot_group, 0)
    slots = start + jnp.arange(slot_group, dtype=jnp.int32)
    live = ((slots >= begin) & (slots < upper)).astype(jnp.float32)
    return (tile_group, row_group, col_group, live)


def forward_tiles(carry, tiles, rows_in, cols_in, piece, first_block, lower, upper):
    edge = tiles.shape[-1]
    blocks = piece.reshape(-1, edge, piece.shape[-1])
    block_count = blocks.shape[0]
    group_total = (upper - lower + slot_group - 1) // slot_group

    def forward_step(group_index, accum):
        begin = lower + group_index * slot_group
        tile_group, row_group, col_group, live = group_slots(tiles, rows_in, cols_in, begin, upper)
        local = jnp.clip(col_group - first_block, 0, block_count - 1)
        taken = jnp.take(blocks, local, axis=0)
        product = jnp.einsum("gij,gjf->gif", tile_group, taken, preferred_element_type=jnp.float32)
        return accum.at[row_group].add(product * live[:, None, None])

    return lax.fori_loop(0, group_total, forward_step, carry)


def backward_tiles(carry, tiles, rows_in, cols_in, grad_blocks, first_block, lower, upper):
    block_count = carry.shape[0]
    group_total = (upper - lower + slot_group - 1) // slot_group

    def backward_step(group_index, accum):
        begin = lower + group_index * slot_group
        tile_group, row_group, col_group, live = group_slots(tiles, rows_in, cols_in, begin, upper)
        taken = jnp.take(grad_blocks, row_group, axis=0)
        product = jnp.einsum("gji,gjf->gif", tile_group, taken, preferred_element_type=jnp.float32)
        local = jnp.clip(col_group - first_block, 0, block_count - 1)
        return accum.at[local].add(product * live[:, None, None])

    return lax.fori_loop(0, group_total, backward_step, carry)


def on_device(
    features, weights, bias_vector, tile_values, tile_rows, tile_cols, tile_counts, cotangent
):
    tiles = tile_values[0, 0]
    rows_in = tile_rows[0, 0]
    cols_in = tile_cols[0, 0]
    live_count = tile_counts[0, 0]
    row_devs = lax.axis_size("row")
    col_devs = lax.axis_size("col")
    local_rows = features.shape[0]
    width = features.shape[1]
    edge = tiles.shape[-1]
    row_tiles = local_rows * col_devs // edge
    col_tiles = local_rows * row_devs // edge
    empty_rows = jnp.zeros((row_tiles, edge, width), jnp.float32)
    column_block = lax.all_gather(features, "row", axis=0, tiled=True)
    lower, upper = tile_range(cols_in, live_count, 0, col_tiles)
    partial_value = forward_tiles(
        empty_rows, tiles, rows_in, cols_in, column_block, 0, lower, upper
    )
    gathered = lax.psum_scatter(
        partial_value.reshape(row_tiles * edge, width).astype(jnp.bfloat16),
        "col",
        scatter_dimension=0,
        tiled=True,
    )
    pre = jnp.dot(gathered, weights, preferred_element_type=jnp.float32) + bias_vector
    sig = jax.nn.sigmoid(pre)
    activated = (pre * sig).astype(jnp.bfloat16)
    dpre = (cotangent.astype(jnp.float32) * sig * (1.0 + pre * (1.0 - sig))).astype(jnp.bfloat16)
    weight_local = lax.dot_general(
        gathered, dpre, (((0,), (0,)), ((), ())), preferred_element_type=jnp.float32
    )
    bias_local = jnp.sum(dpre.astype(jnp.float32), axis=0)
    weight_total, bias_total = lax.psum((weight_local, bias_local), ("row", "col"))
    scale = 1.0 / math.sqrt(local_rows * row_devs * col_devs)
    weight_grad = weight_total * scale
    bias_grad = bias_total * scale
    dgathered = lax.dot_general(
        dpre, weights, (((1,), (1,)), ((), ())), preferred_element_type=jnp.float32
    ).astype(jnp.bfloat16)
    row_block = lax.all_gather(dgathered, "col", axis=0, tiled=True)
    grad_blocks = row_block.reshape(row_tiles, edge, width)
    lower, upper = tile_range(cols_in, live_count, 0, col_tiles)
    empty_cols = jnp.zeros((col_tiles, edge, width), jnp.float32)
    term = backward_tiles(empty_cols, tiles, rows_in, cols_in, grad_blocks, 0, lower, upper)
    feature_sum = lax.psum_scatter(
        term.reshape(col_tiles * edge, width).astype(jnp.bfloat16),
        "row",
        scatter_dimension=0,
        tiled=True,
    )
    return (activated, weight_grad, bias_grad, feature_sum)


MESH = pl.DeviceIdType.MESH


def densify(tiles, rows_in, cols_in, live_count, row_tiles, col_tiles, wide):
    slots, edge = tiles.shape[0], tiles.shape[-1]
    per_step = wide // edge
    steps = col_tiles // per_step

    def body(rows_ref, cols_ref, count_ref, tiles_ref, out_ref, accum, cursor):
        step = pl.program_id(0)

        @pl.when(step == 0)
        def _():
            cursor[0] = 0

        count = count_ref[0]
        for part in range(per_step):
            column = step * per_step + part
            accum[...] = jnp.zeros_like(accum)

            def more(slot):
                return (slot < count) & (cols_ref[jnp.minimum(slot, slots - 1)] == column)

            def add(slot):
                window = pl.ds(pl.multiple_of(rows_ref[slot] * edge, edge), edge)
                accum[window, :] += tiles_ref[slot].astype(jnp.float32)
                return slot + 1

            cursor[0] = lax.while_loop(more, add, cursor[0])
            out_ref[0, :, part * edge : (part + 1) * edge] = accum[...].astype(jnp.bfloat16)

    return pl.pallas_call(
        body,
        out_shape=jax.ShapeDtypeStruct((steps, row_tiles * edge, wide), jnp.bfloat16),
        grid_spec=pltpu.PrefetchScalarGridSpec(
            num_scalar_prefetch=3,
            grid=(steps,),
            in_specs=[
                pl.BlockSpec(
                    tiles.shape, lambda s, *_: (0, 0, 0), pipeline_mode=pl.Buffered(1)
                )
            ],
            out_specs=pl.BlockSpec((1, row_tiles * edge, wide), lambda s, *_: (s, 0, 0)),
            scratch_shapes=[
                pltpu.VMEM((row_tiles * edge, edge), jnp.float32),
                pltpu.SMEM((1,), jnp.int32),
            ],
        ),
        compiler_params=pltpu.CompilerParams(vmem_limit_bytes=24 << 20),
    )(rows_in, cols_in, live_count, tiles)


def layer_kernel(
    Z, FC, scale,
    a_hbm, x_ref, w_ref, b_ref, cot_ref,
    act_ref, wg_ref, bg_ref, fg_ref,
    av, xg, acc, psend, precv, gath, dpre_s, dg,
    own, sbuf, srecv, csend, crecv,
    fsum, wl, wra, wa, wrb, wb, wrc, wfin, bs, br, br2,
    a_sem, gz_s, gz_r, gs_s, gs_r, p_s, p_r, d_s, d_r,
    s_s, s_r, c_s, c_r, w_s, w_r, wz_s, wz_r, wf_s, wf_r, bz_s, bz_r, bx_s, bx_r,
):
    r = lax.axis_index("row")
    c = lax.axis_index("col")
    z, k = r // 2, r % 2
    V, F = x_ref.shape
    fc = F // FC
    f32, bf16 = jnp.float32, jnp.bfloat16
    sib = {"row": z * 2 + (1 - k)}
    peer = {"col": 1 - c}

    def at_z(t):
        return {"row": t * 2 + k}

    def rc(src, dst, ss, rs, dev):
        return pltpu.make_async_remote_copy(
            src_ref=src, dst_ref=dst, send_sem=ss, recv_sem=rs, device_id=dev, device_id_type=MESH
        )

    def got(dst, rs):
        rc(dst, dst, d_s.at[0], rs, sib).wait_recv()

    for s in range(2 * Z):
        pltpu.make_async_copy(a_hbm.at[s], av.at[s], a_sem.at[s]).start()

    barrier = pltpu.get_barrier_semaphore()
    pl.semaphore_signal(barrier, inc=1, device_id=sib, device_id_type=MESH)
    pl.semaphore_signal(barrier, inc=1, device_id=peer, device_id_type=MESH)
    for off in range(1, Z):
        pl.semaphore_signal(barrier, inc=1, device_id=at_z((z + off) % Z), device_id_type=MESH)
    for h in range(FC):
        xg[h, z, k] = x_ref[:, h * fc : (h + 1) * fc]
    pl.semaphore_wait(barrier, Z + 1)

    def z_copy(h, t, step):
        slot = xg.at[h, t, k]
        return rc(slot, slot, gz_s.at[h, (1 - step) // 2, t], gz_r.at[h, t], at_z(z + step))

    def s_copy(h, t):
        slot = xg.at[h, t, k]
        return rc(slot, slot, gs_s.at[h, t], gs_r.at[h, t], sib)

    def own_sends(h):
        @pl.when(z < Z - 1)
        def _():
            z_copy(h, z, 1).start()

        @pl.when(z > 0)
        def _():
            z_copy(h, z, -1).start()

        s_copy(h, z).start()

    def mm(h, t, plane, first=False):
        s = t * 2 + plane
        if h == 0:
            pltpu.make_async_copy(a_hbm.at[s], av.at[s], a_sem.at[s]).wait()
        prod = jnp.dot(av[s], xg[h, t, plane], preferred_element_type=f32)
        if first:
            acc[h] = prod
        else:
            acc[h] += prod

    def p_copy(h):
        return rc(psend.at[h], precv.at[h], p_s.at[h], p_r.at[h], peer)

    own_sends(0)
    for h in range(FC):
        mm(h, z, k, True)
        got(xg.at[h, z, 1 - k], gs_r.at[h, z])
        mm(h, z, 1 - k)
        for dist in range(1, Z):
            sides = ((z - dist, z - dist >= 0, 1), (z + dist, z + dist < Z, -1))
            for t, valid, step in sides:

                @pl.when(valid)
                def _(t=t, step=step):
                    got(xg.at[h, t, k], gz_r.at[h, t])

                    @pl.when((z + step >= 0) & (z + step < Z))
                    def _():
                        z_copy(h, t, step).start()

                    s_copy(h, t).start()

            if dist == max(Z - 2, 1) and h + 1 < FC:
                own_sends(h + 1)
            for t, valid, step in sides:

                @pl.when(valid)
                def _(t=t):
                    mm(h, t, k)
                    got(xg.at[h, t, 1 - k], gs_r.at[h, t])
                    mm(h, t, 1 - k)

        psend[h] = acc[h, pl.ds(pl.multiple_of((1 - c) * V, V), V), :].astype(bf16)
        p_copy(h).start()

    pre = jnp.broadcast_to(b_ref[...], (V, F))
    for h in range(FC):
        p_copy(h).wait_recv()
        g = acc[h, pl.ds(pl.multiple_of(c * V, V), V), :] + precv[h].astype(f32)
        gath[:, h * fc : (h + 1) * fc] = g.astype(bf16)
        pre = pre + jnp.dot(
            g.astype(bf16), w_ref[h * fc : (h + 1) * fc, :], preferred_element_type=f32
        )
    sig = jax.nn.sigmoid(pre)
    act_ref[...] = (pre * sig).astype(bf16)
    dval = (cot_ref[...].astype(f32) * sig * (1.0 + pre * (1.0 - sig))).astype(bf16)
    dpre_s[...] = dval

    def d_copy(h):
        slot = dg.at[h, c]
        return rc(slot, slot, d_s.at[h], d_r.at[h], peer)

    for h in range(FC):
        dg[h, c] = lax.dot_general(
            w_ref[h * fc : (h + 1) * fc, :], dpre_s[...], (((1,), (1,)), ((), ())),
            preferred_element_type=f32,
        ).astype(bf16)
        d_copy(h).start()

    bs[0] = jnp.sum(dpre_s[...].astype(f32).reshape(V // 8, 8, F), axis=0)
    wl[...] = lax.dot_general(
        gath[...], dpre_s[...], (((0,), (0,)), ((), ())), preferred_element_type=f32
    )
    H, Q, P8 = F // 2, F // 4, F // (4 * Z)
    wa_copy = rc(wl.at[pl.ds(pl.multiple_of((1 - k) * H, H), H), :], wra, w_s.at[0], w_r.at[0], sib)
    ba_copy = rc(bs.at[0], br.at[0], bx_s.at[0], bx_r.at[0], sib)
    wb_copy = rc(wa.at[pl.ds(pl.multiple_of((1 - c) * Q, Q), Q), :], wrb, w_s.at[1], w_r.at[1], peer)
    bb_copy = rc(bs.at[1], br.at[1], bx_s.at[1], bx_r.at[1], peer)
    we_copy = rc(wfin.at[k, c], wfin.at[k, c], w_s.at[2], w_r.at[2], peer)
    wf_copy = rc(wfin.at[k], wfin.at[k], w_s.at[3], w_r.at[3], sib)

    def wc_copy(off):
        t = (z + off) % Z
        return rc(wb.at[t], wrc.at[off], wz_s.at[off], wz_r.at[off], at_z(t))

    def wd_copy(off):
        t = (z + off) % Z
        return rc(wfin.at[k, c, z], wfin.at[k, c, z], wf_s.at[off], wf_r.at[off], at_z(t))

    def bc_copy(off):
        t = (z + off) % Z
        return rc(bs.at[2], br2.at[off], bz_s.at[off], bz_r.at[off], at_z(t))

    wa_copy.start()
    ba_copy.start()

    def stage_b():
        wa_copy.wait_recv()
        ba_copy.wait_recv()
        wa[...] = wl[pl.ds(pl.multiple_of(k * H, H), H), :] + wra[...]
        bs[1] = bs[0] + br[0]
        wb_copy.start()
        bb_copy.start()

    def stage_c():
        wb_copy.wait_recv()
        bb_copy.wait_recv()
        both = wa[pl.ds(pl.multiple_of(c * Q, Q), Q), :] + wrb[...]
        wb[...] = both.astype(bf16).reshape(Z, P8, F)
        bs[2] = bs[1] + br[1]
        for off in range(1, Z):
            wc_copy(off).start()
            bc_copy(off).start()

    def stage_d():
        total = wb[z].astype(f32)
        btotal = bs[2]
        for off in range(1, Z):
            wc_copy(off).wait_recv()
            bc_copy(off).wait_recv()
            total = total + wrc[off].astype(f32)
            btotal = btotal + br2[off]
        wfin[k, c, z] = (total * scale).astype(bf16)
        bg_ref[...] = btotal * scale
        for off in range(1, Z):
            wd_copy(off).start()

    def stage_e():
        for off in range(1, Z):
            t = (z - off + Z) % Z
            got(wfin.at[k, c, t], wf_r.at[off])
        we_copy.start()

    def stage_f():
        got(wfin.at[k, 1 - c], w_r.at[2])
        wf_copy.start()

    def s2_copy(h, d):
        return rc(sbuf.at[h, d], srecv.at[h, d], s_s.at[h, d], s_r.at[h, d], sib)

    def c_copy(h, d, way):
        step = 1 if way == 0 else -1
        return rc(
            csend.at[h, d], crecv.at[h, d, way], c_s.at[h, d], c_r.at[h, d, way], at_z(z + step)
        )

    def bmm(h, d, plane):
        s = d * 2 + plane
        total = jnp.dot(dg[h, 0], av[s, :V, :], preferred_element_type=f32)
        total = total + jnp.dot(dg[h, 1], av[s, V:, :], preferred_element_type=f32)
        return total.astype(bf16)

    def compute(h):
        got(dg.at[h, 1 - c], d_r.at[h])

        def one(i, carry):
            d = jnp.where(z * 2 < Z, Z - 1 - i, i)
            sbuf[h, d] = bmm(h, d, 1 - k)
            s2_copy(h, d).start()
            own[h, d] = bmm(h, d, k)
            return carry

        lax.fori_loop(0, Z, one, 0)

    def local_sum(h, d):
        s2_copy(h, d).wait_recv()
        return own[h, d].astype(f32) + srecv[h, d].astype(f32)

    def chain(h):
        for dist in range(Z - 1, 0, -1):
            for way, d, valid, inner in (
                (0, z + dist, z + dist < Z, z > 0),
                (1, z - dist, z - dist >= 0, z < Z - 1),
            ):

                @pl.when(valid & inner)
                def _(way=way, d=d):
                    total = local_sum(h, d)
                    got(crecv.at[h, d, way], c_r.at[h, d, way])
                    csend[h, d] = (total + crecv[h, d, way].astype(f32)).astype(bf16)
                    c_copy(h, d, way).start()

                @pl.when(valid & jnp.logical_not(inner))
                def _(way=way, d=d):
                    csend[h, d] = local_sum(h, d).astype(bf16)
                    c_copy(h, d, way).start()

    def finish(h):
        s2_copy(h, z).wait_recv()
        fsum[...] = own[h, z].astype(f32) + srecv[h, z].astype(f32)

        @pl.when(z > 0)
        def _():
            got(crecv.at[h, z, 0], c_r.at[h, z, 0])
            fsum[...] += crecv[h, z, 0].astype(f32)

        @pl.when(z < Z - 1)
        def _():
            got(crecv.at[h, z, 1], c_r.at[h, z, 1])
            fsum[...] += crecv[h, z, 1].astype(f32)

        fg_ref[:, h * fc : (h + 1) * fc] = fsum[...].T.astype(bf16)

    compute(0)
    stage_b()
    for h in range(1, FC):
        compute(h)
    stage_c()
    chain(0)
    stage_d()
    for h in range(1, FC):
        chain(h)
    stage_e()
    for h in range(FC - 1):
        finish(h)
    stage_f()
    finish(FC - 1)
    got(wfin.at[1 - k], w_r.at[3])
    wg_ref[...] = wfin[...].astype(f32).reshape(F, F)

    for h in range(FC):
        for t in range(Z):

            @pl.when((z < Z - 1) & (t <= z))
            def _(t=t):
                z_copy(h, t, 1).wait_send()

            @pl.when((z > 0) & (t >= z))
            def _(t=t):
                z_copy(h, t, -1).wait_send()

            s_copy(h, t).wait_send()
            s2_copy(h, t).wait_send()

            @pl.when(t > z)
            def _(t=t):
                c_copy(h, t, 0).wait_send()

            @pl.when(t < z)
            def _(t=t):
                c_copy(h, t, 1).wait_send()

        p_copy(h).wait_send()
        d_copy(h).wait_send()
    for copy in (wa_copy, ba_copy, wb_copy, bb_copy, we_copy, wf_copy):
        copy.wait_send()
    for off in range(1, Z):
        wc_copy(off).wait_send()
        bc_copy(off).wait_send()
        wd_copy(off).wait_send()


def fused_layer(adjacency, features, weights, bias_vector, cotangent, Z, FC):
    V, F = features.shape
    R, fc = 2 * Z, F // FC
    f32, bf16 = jnp.float32, jnp.bfloat16
    H, Q, P8 = F // 2, F // 4, F // (4 * Z)
    dma = pltpu.SemaphoreType.DMA
    vm = pltpu.VMEM
    scale = 1.0 / math.sqrt(V * R * 2)
    whole = pl.BlockSpec(memory_space=pltpu.VMEM)
    return pl.pallas_call(
        functools.partial(layer_kernel, Z, FC, scale),
        out_shape=(
            jax.ShapeDtypeStruct((V, F), bf16),
            jax.ShapeDtypeStruct((F, F), f32),
            jax.ShapeDtypeStruct((8, F), f32),
            jax.ShapeDtypeStruct((V, F), bf16),
        ),
        in_specs=[pl.BlockSpec(memory_space=pl.ANY)] + [whole] * 4,
        out_specs=[whole] * 4,
        scratch_shapes=[
            vm((R, 2 * V, V), bf16), vm((FC, Z, 2, V, fc), bf16), vm((FC, 2 * V, fc), f32),
            vm((FC, V, fc), bf16), vm((FC, V, fc), bf16), vm((V, F), bf16), vm((V, F), bf16),
            vm((FC, 2, fc, V), bf16),
            vm((FC, Z, fc, V), bf16), vm((FC, Z, fc, V), bf16), vm((FC, Z, fc, V), bf16),
            vm((FC, Z, fc, V), bf16), vm((FC, Z, 2, fc, V), bf16),
            vm((fc, V), f32), vm((F, F), f32), vm((H, F), f32), vm((H, F), f32), vm((Q, F), f32),
            vm((Z, P8, F), bf16), vm((Z, P8, F), bf16), vm((2, 2, Z, P8, F), bf16),
            vm((3, 8, F), f32), vm((2, 8, F), f32), vm((Z, 8, F), f32),
            dma((R,)), dma((FC, 2, Z)), dma((FC, Z)), dma((FC, Z)), dma((FC, Z)),
            dma((FC,)), dma((FC,)), dma((FC,)), dma((FC,)),
            dma((FC, Z)), dma((FC, Z)), dma((FC, Z)), dma((FC, Z, 2)),
            dma((4,)), dma((4,)), dma((Z,)), dma((Z,)), dma((Z,)), dma((Z,)),
            dma((Z,)), dma((Z,)), dma((2,)), dma((2,)),
        ],
        compiler_params=pltpu.CompilerParams(
            collective_id=0, has_side_effects=True, vmem_limit_bytes=60 << 20
        ),
    )(adjacency, features, weights, bias_vector.reshape(1, F), cotangent)


def on_device_fused(
    features, weights, bias_vector, tile_values, tile_rows, tile_cols, tile_counts, cotangent
):
    tiles = tile_values[0, 0]
    rows = lax.axis_size("row")
    local_rows, edge = features.shape[0], tiles.shape[-1]
    adjacency = densify(
        tiles, tile_rows[0, 0], tile_cols[0, 0], tile_counts[0],
        local_rows * 2 // edge, local_rows * rows // edge, local_rows,
    )
    activated, weight_grad, bias_rows, feature_grad = fused_layer(
        adjacency, features, weights, bias_vector, cotangent, rows // 2, feature_chunks
    )
    return (activated, weight_grad, jnp.sum(bias_rows, axis=0), feature_grad)


def solution(mesh):
    in_specs = (
        P(("rep", "col", "row"), None),
        P(),
        P(),
        P(("rep", "row"), "col", None, None, None),
        P(("rep", "row"), "col", None),
        P(("rep", "row"), "col", None),
        P(("rep", "row"), "col"),
        P(("rep", "row", "col"), None),
    )
    out_specs = (
        P(("rep", "row", "col"), None),
        P("rep", None),
        P("rep"),
        P(("rep", "col", "row"), None),
    )
    small = mesh.shape["col"] == 2 and mesh.shape["row"] % 2 == 0
    return jax.shard_map(
        on_device_fused if small else on_device, mesh=mesh, in_specs=in_specs, out_specs=out_specs, check_vma=False
    )
```

```python
import functools
import math

import jax
import jax.numpy as jnp
from jax import lax
from jax.experimental import pallas as pl
from jax.experimental.pallas import tpu as pltpu
from jax.sharding import PartitionSpec as P

slot_group = 16
feature_chunks = 2


def tile_range(cols_in, live_count, first_block, last_block):
    slots = jnp.arange(cols_in.shape[0], dtype=jnp.int32)
    live = slots < live_count
    lower = jnp.sum((live & (cols_in < first_block)).astype(jnp.int32))
    upper = jnp.sum((live & (cols_in < last_block)).astype(jnp.int32))
    return (lower, upper)


def group_slots(tiles, rows_in, cols_in, begin, upper):
    limit = tiles.shape[0] - slot_group
    start = jnp.minimum(begin, limit)
    tile_group = lax.dynamic_slice_in_dim(tiles, start, slot_group, 0)
    row_group = lax.dynamic_slice_in_dim(rows_in, start, slot_group, 0)
    col_group = lax.dynamic_slice_in_dim(cols_in, start, slot_group, 0)
    slots = start + jnp.arange(slot_group, dtype=jnp.int32)
    live = ((slots >= begin) & (slots < upper)).astype(jnp.float32)
    return (tile_group, row_group, col_group, live)


def forward_tiles(carry, tiles, rows_in, cols_in, piece, first_block, lower, upper):
    edge = tiles.shape[-1]
    blocks = piece.reshape(-1, edge, piece.shape[-1])
    block_count = blocks.shape[0]
    group_total = (upper - lower + slot_group - 1) // slot_group

    def forward_step(group_index, accum):
        begin = lower + group_index * slot_group
        tile_group, row_group, col_group, live = group_slots(tiles, rows_in, cols_in, begin, upper)
        local = jnp.clip(col_group - first_block, 0, block_count - 1)
        taken = jnp.take(blocks, local, axis=0)
        product = jnp.einsum("gij,gjf->gif", tile_group, taken, preferred_element_type=jnp.float32)
        return accum.at[row_group].add(product * live[:, None, None])

    return lax.fori_loop(0, group_total, forward_step, carry)


def backward_tiles(carry, tiles, rows_in, cols_in, grad_blocks, first_block, lower, upper):
    block_count = carry.shape[0]
    group_total = (upper - lower + slot_group - 1) // slot_group

    def backward_step(group_index, accum):
        begin = lower + group_index * slot_group
        tile_group, row_group, col_group, live = group_slots(tiles, rows_in, cols_in, begin, upper)
        taken = jnp.take(grad_blocks, row_group, axis=0)
        product = jnp.einsum("gji,gjf->gif", tile_group, taken, preferred_element_type=jnp.float32)
        local = jnp.clip(col_group - first_block, 0, block_count - 1)
        return accum.at[local].add(product * live[:, None, None])

    return lax.fori_loop(0, group_total, backward_step, carry)


def on_device(
    features, weights, bias_vector, tile_values, tile_rows, tile_cols, tile_counts, cotangent
):
    tiles = tile_values[0, 0]
    rows_in = tile_rows[0, 0]
    cols_in = tile_cols[0, 0]
    live_count = tile_counts[0, 0]
    row_devs = lax.axis_size("row")
    col_devs = lax.axis_size("col")
    local_rows = features.shape[0]
    width = features.shape[1]
    edge = tiles.shape[-1]
    row_tiles = local_rows * col_devs // edge
    col_tiles = local_rows * row_devs // edge
    empty_rows = jnp.zeros((row_tiles, edge, width), jnp.float32)
    column_block = lax.all_gather(features, "row", axis=0, tiled=True)
    lower, upper = tile_range(cols_in, live_count, 0, col_tiles)
    partial_value = forward_tiles(
        empty_rows, tiles, rows_in, cols_in, column_block, 0, lower, upper
    )
    gathered = lax.psum_scatter(
        partial_value.reshape(row_tiles * edge, width).astype(jnp.bfloat16),
        "col",
        scatter_dimension=0,
        tiled=True,
    )
    pre = jnp.dot(gathered, weights, preferred_element_type=jnp.float32) + bias_vector
    sig = jax.nn.sigmoid(pre)
    activated = (pre * sig).astype(jnp.bfloat16)
    dpre = (cotangent.astype(jnp.float32) * sig * (1.0 + pre * (1.0 - sig))).astype(jnp.bfloat16)
    weight_local = lax.dot_general(
        gathered, dpre, (((0,), (0,)), ((), ())), preferred_element_type=jnp.float32
    )
    bias_local = jnp.sum(dpre.astype(jnp.float32), axis=0)
    weight_total, bias_total = lax.psum((weight_local, bias_local), ("row", "col"))
    scale = 1.0 / math.sqrt(local_rows * row_devs * col_devs)
    weight_grad = weight_total * scale
    bias_grad = bias_total * scale
    dgathered = lax.dot_general(
        dpre, weights, (((1,), (1,)), ((), ())), preferred_element_type=jnp.float32
    ).astype(jnp.bfloat16)
    row_block = lax.all_gather(dgathered, "col", axis=0, tiled=True)
    grad_blocks = row_block.reshape(row_tiles, edge, width)
    lower, upper = tile_range(cols_in, live_count, 0, col_tiles)
    empty_cols = jnp.zeros((col_tiles, edge, width), jnp.float32)
    term = backward_tiles(empty_cols, tiles, rows_in, cols_in, grad_blocks, 0, lower, upper)
    feature_sum = lax.psum_scatter(
        term.reshape(col_tiles * edge, width).astype(jnp.bfloat16),
        "row",
        scatter_dimension=0,
        tiled=True,
    )
    return (activated, weight_grad, bias_grad, feature_sum)


MESH = pl.DeviceIdType.MESH


def densify(tiles, rows_in, cols_in, live_count, row_tiles, col_tiles, wide):
    slots, edge = tiles.shape[0], tiles.shape[-1]
    per_step = wide // edge
    steps = col_tiles // per_step

    pieces = slots // slot_group

    def body(rows_ref, cols_ref, count_ref, tiles_hbm, out_ref, tiles_ref, accum, cursor, sems):
        step = pl.program_id(0)
        count = count_ref[0]

        def piece_copy(piece):
            window = pl.ds(piece * slot_group, slot_group)
            return pltpu.make_async_copy(tiles_hbm.at[window], tiles_ref.at[window], sems.at[piece])

        @pl.when(step == 0)
        def _():
            cursor[0] = 0
            for piece in range(pieces):

                @pl.when(piece * slot_group < count)
                def _(piece=piece):
                    piece_copy(piece).start()

        for part in range(per_step):
            column = step * per_step + part
            accum[...] = jnp.zeros_like(accum)

            def more(slot):
                return (slot < count) & (cols_ref[jnp.minimum(slot, slots - 1)] == column)

            def add(slot):
                @pl.when(slot % slot_group == 0)
                def _():
                    piece_copy(slot // slot_group).wait()

                window = pl.ds(pl.multiple_of(rows_ref[slot] * edge, edge), edge)
                accum[window, :] += tiles_ref[slot].astype(jnp.float32)
                return slot + 1

            cursor[0] = lax.while_loop(more, add, cursor[0])
            out_ref[0, :, part * edge : (part + 1) * edge] = accum[...].astype(jnp.bfloat16)

    return pl.pallas_call(
        body,
        out_shape=jax.ShapeDtypeStruct((steps, row_tiles * edge, wide), jnp.bfloat16),
        grid_spec=pltpu.PrefetchScalarGridSpec(
            num_scalar_prefetch=3,
            grid=(steps,),
            in_specs=[pl.BlockSpec(memory_space=pltpu.HBM)],
            out_specs=pl.BlockSpec((1, row_tiles * edge, wide), lambda s, *_: (s, 0, 0)),
            scratch_shapes=[
                pltpu.VMEM(tiles.shape, tiles.dtype),
                pltpu.VMEM((row_tiles * edge, edge), jnp.float32),
                pltpu.SMEM((1,), jnp.int32),
                pltpu.SemaphoreType.DMA((pieces,)),
            ],
        ),
        compiler_params=pltpu.CompilerParams(vmem_limit_bytes=12 << 20),
    )(rows_in, cols_in, live_count, tiles)


def layer_kernel(
    Z, FC, scale,
    a_hbm, x_ref, w_ref, b_ref, cot_ref,
    act_ref, wg_ref, bg_ref, fg_ref,
    av, xg, acc, psend, precv, gath, dpre_s, dg,
    own, sbuf, srecv, csend, crecv, cmid,
    fsum, wl, wra, wa, wab, wrb, wb, wrc, wfin, bs, br, br2,
    a_sem, gz_s, gz_r, gs_s, gs_r, p_s, p_r, d_s, d_r,
    s_s, s_r, c_s, c_r, m_r, w_s, w_r, wz_s, wz_r, wf_s, wf_r, bz_s, bz_r, bx_s, bx_r,
):
    r = lax.axis_index("row")
    c = lax.axis_index("col")
    z, k = r // 2, r % 2
    V, F = x_ref.shape
    fc = F // FC
    f32, bf16 = jnp.float32, jnp.bfloat16
    sib = {"row": z * 2 + (1 - k)}
    peer = {"col": 1 - c}

    def at_z(t):
        return {"row": t * 2 + k}

    def rc(src, dst, ss, rs, dev):
        return pltpu.make_async_remote_copy(
            src_ref=src, dst_ref=dst, send_sem=ss, recv_sem=rs, device_id=dev, device_id_type=MESH
        )

    def got(dst, rs):
        rc(dst, dst, d_s.at[0], rs, sib).wait_recv()

    for s in range(2 * Z):
        pltpu.make_async_copy(a_hbm.at[s], av.at[s], a_sem.at[s]).start()

    barrier = pltpu.get_barrier_semaphore()
    pl.semaphore_signal(barrier, inc=1, device_id=sib, device_id_type=MESH)
    pl.semaphore_signal(barrier, inc=1, device_id=peer, device_id_type=MESH)
    for off in range(1, Z):
        pl.semaphore_signal(barrier, inc=1, device_id=at_z((z + off) % Z), device_id_type=MESH)
    for h in range(FC):
        xg[h, z, k] = x_ref[:, h * fc : (h + 1) * fc]
    pl.semaphore_wait(barrier, Z + 1)

    end = (z == 0) | (z == Z - 1)

    def mirrored(position):
        return jnp.where(z * 2 < Z, position, Z - 1 - position)

    def z_copy(h, t, dst, kind):
        slot = xg.at[h, t, k]
        return rc(slot, slot, gz_s.at[h, kind, dst], gz_r.at[h, t], at_z(dst))

    def s_copy(h, t):
        slot = xg.at[h, t, k]
        return rc(slot, slot, gs_s.at[h, t], gs_r.at[h, t], sib)

    def own_targets(h, act):
        @pl.when(end)
        def _():
            for position in (3, 2, 1):
                act(z_copy(h, z, mirrored(position), 0))

        @pl.when(jnp.logical_not(end))
        def _():
            for position in (2, 0):
                act(z_copy(h, z, mirrored(position), 0))

    def own_sends(h):
        own_targets(h, lambda copy: copy.start())
        s_copy(h, z).start()

    def mm(h, t, plane, first=False):
        s = t * 2 + plane
        if h == 0:
            pltpu.make_async_copy(a_hbm.at[s], av.at[s], a_sem.at[s]).wait()
        prod = jnp.dot(av[s], xg[h, t, plane], preferred_element_type=f32)
        if first:
            acc[h] = prod
        else:
            acc[h] += prod

    def p_copy(h):
        return rc(psend.at[h], precv.at[h], p_s.at[h], p_r.at[h], peer)

    own_sends(0)
    for h in range(FC):
        mm(h, z, k, True)
        got(xg.at[h, z, 1 - k], gs_r.at[h, z])
        mm(h, z, 1 - k)
        for turn in range(Z - 1):
            t = mirrored(jnp.where(end, (1, 3, 2)[turn], (2, 0, 3)[turn]))
            got(xg.at[h, t, k], gz_r.at[h, t])
            if turn == 0:

                @pl.when(jnp.logical_not(end))
                def _(t=t):
                    z_copy(h, t, mirrored(0), 1).start()

            s_copy(h, t).start()
            if turn == 0 and h + 1 < FC:
                own_sends(h + 1)
            mm(h, t, k)
            got(xg.at[h, t, 1 - k], gs_r.at[h, t])
            mm(h, t, 1 - k)

        psend[h] = acc[h, pl.ds(pl.multiple_of((1 - c) * V, V), V), :].astype(bf16)
        p_copy(h).start()

    pre = jnp.broadcast_to(b_ref[...], (V, F))
    for h in range(FC):
        p_copy(h).wait_recv()
        g = acc[h, pl.ds(pl.multiple_of(c * V, V), V), :] + precv[h].astype(f32)
        gath[:, h * fc : (h + 1) * fc] = g.astype(bf16)
        pre = pre + jnp.dot(
            g.astype(bf16), w_ref[h * fc : (h + 1) * fc, :], preferred_element_type=f32
        )
    sig = jax.nn.sigmoid(pre)
    act_ref[...] = (pre * sig).astype(bf16)
    dval = (cot_ref[...].astype(f32) * sig * (1.0 + pre * (1.0 - sig))).astype(bf16)
    dpre_s[...] = dval

    def d_copy(h):
        slot = dg.at[h, c]
        return rc(slot, slot, d_s.at[h], d_r.at[h], peer)

    for h in range(FC):
        dg[h, c] = lax.dot_general(
            w_ref[h * fc : (h + 1) * fc, :], dpre_s[...], (((1,), (1,)), ((), ())),
            preferred_element_type=f32,
        ).astype(bf16)
        d_copy(h).start()

    bs[0] = jnp.sum(dpre_s[...].astype(f32).reshape(V // 8, 8, F), axis=0)
    wl[...] = lax.dot_general(
        gath[...], dpre_s[...], (((0,), (0,)), ((), ())), preferred_element_type=f32
    )
    H, Q, P8 = F // 2, F // 4, F // (4 * Z)
    wa_copy = rc(wl.at[pl.ds(pl.multiple_of((1 - k) * H, H), H), :], wra, w_s.at[0], w_r.at[0], sib)
    ba_copy = rc(bs.at[0], br.at[0], bx_s.at[0], bx_r.at[0], sib)
    wb_copy = rc(wab, wrb, w_s.at[1], w_r.at[1], peer)
    bb_copy = rc(bs.at[1], br.at[1], bx_s.at[1], bx_r.at[1], peer)
    we_copy = rc(wfin.at[k, c], wfin.at[k, c], w_s.at[2], w_r.at[2], peer)
    wf_copy = rc(wfin.at[k], wfin.at[k], w_s.at[3], w_r.at[3], sib)

    def wc_copy(off):
        t = (z + off) % Z
        return rc(wb.at[t], wrc.at[off], wz_s.at[off], wz_r.at[off], at_z(t))

    def wd_copy(off):
        t = (z + off) % Z
        return rc(wfin.at[k, c, z], wfin.at[k, c, z], wf_s.at[off], wf_r.at[off], at_z(t))

    def bc_copy(off):
        t = (z + off) % Z
        return rc(bs.at[2], br2.at[off], bz_s.at[off], bz_r.at[off], at_z(t))

    wa_copy.start()
    ba_copy.start()

    def stage_b():
        wa_copy.wait_recv()
        ba_copy.wait_recv()
        wa[...] = wl[pl.ds(pl.multiple_of(k * H, H), H), :] + wra[...]
        wab[...] = wa[pl.ds(pl.multiple_of((1 - c) * Q, Q), Q), :].astype(bf16)
        bs[1] = bs[0] + br[0]
        wb_copy.start()
        bb_copy.start()

    def stage_c():
        wb_copy.wait_recv()
        bb_copy.wait_recv()
        both = wa[pl.ds(pl.multiple_of(c * Q, Q), Q), :] + wrb[...].astype(f32)
        wb[...] = both.astype(bf16).reshape(Z, P8, F)
        bs[2] = bs[1] + br[1]
        for off in range(1, Z):
            wc_copy(off).start()
            bc_copy(off).start()

    def stage_d():
        total = wb[z].astype(f32)
        btotal = bs[2]
        for off in range(1, Z):
            wc_copy(off).wait_recv()
            bc_copy(off).wait_recv()
            total = total + wrc[off].astype(f32)
            btotal = btotal + br2[off]
        wfin[k, c, z] = (total * scale).astype(bf16)
        bg_ref[...] = jnp.sum(btotal, axis=0, keepdims=True) * scale
        for off in range(1, Z):
            wd_copy(off).start()

    def stage_e():
        for off in range(1, Z):
            t = (z - off + Z) % Z
            got(wfin.at[k, c, t], wf_r.at[off])
        we_copy.start()

    def stage_f():
        got(wfin.at[k, 1 - c], w_r.at[2])
        wf_copy.start()

    def s2_copy(h, d):
        return rc(sbuf.at[h, d], srecv.at[h, d], s_s.at[h, d], s_r.at[h, d], sib)

    def c_copy(h, d):
        return rc(csend.at[h, d], crecv.at[h, z], c_s.at[h, d], c_r.at[h, z], at_z(d))

    def mid_copy(h):
        return rc(
            csend.at[h, Z - 1 - z], cmid.at[h], c_s.at[h, Z - 1 - z], m_r.at[h], at_z(mirrored(1))
        )

    def bmm(h, d, plane):
        s = d * 2 + plane
        total = jnp.dot(dg[h, 0], av[s, :V, :], preferred_element_type=f32)
        total = total + jnp.dot(dg[h, 1], av[s, V:, :], preferred_element_type=f32)
        return total.astype(bf16)

    def target(i):
        return mirrored(jnp.where(end, Z - 1 - i, (i + 2) % Z))

    def local_sum(h, d):
        s2_copy(h, d).wait_recv()
        return own[h, d].astype(f32) + srecv[h, d].astype(f32)

    def ship(h, i):
        d = target(i)

        @pl.when(end | (i != 1))
        def _():
            csend[h, d] = local_sum(h, d).astype(bf16)

        @pl.when(end & (i == 0))
        def _():
            mid_copy(h).start()

        @pl.when((end & (i != 0)) | (jnp.logical_not(end) & (i != 1)))
        def _():
            c_copy(h, d).start()

    def products(i, carry):
        d = target(i)
        for h in range(FC):

            @pl.when(i == 0)
            def _(h=h):
                got(dg.at[h, 1 - c], d_r.at[h])

            sbuf[h, d] = bmm(h, d, 1 - k)
            s2_copy(h, d).start()
            own[h, d] = bmm(h, d, k)

            @pl.when(i > 0)
            def _(h=h):
                ship(h, i - 1)

        return carry

    def middle(h):
        @pl.when(jnp.logical_not(end))
        def _():
            d = target(1)
            got(cmid.at[h], m_r.at[h])
            csend[h, d] = (local_sum(h, d) + cmid[h].astype(f32)).astype(bf16)
            c_copy(h, d).start()

    def finish(h):
        s2_copy(h, z).wait_recv()
        fsum[...] = own[h, z].astype(f32) + srecv[h, z].astype(f32)

        for src in range(Z):

            @pl.when((z != src) & jnp.logical_not(end & (z == Z - 1 - src)))
            def _(src=src):
                got(crecv.at[h, src], c_r.at[h, src])
                fsum[...] += crecv[h, src].astype(f32)

        fg_ref[:, h * fc : (h + 1) * fc] = fsum[...].T.astype(bf16)

    lax.fori_loop(0, Z, products, 0)
    stage_b()
    for h in range(FC):
        middle(h)
    stage_c()
    for h in range(FC - 1):
        finish(h)
    stage_d()
    stage_e()
    finish(FC - 1)
    stage_f()
    got(wfin.at[1 - k], w_r.at[3])
    wg_ref[...] = wfin[...].reshape(F, F)

    for h in range(FC):
        own_targets(h, lambda copy: copy.wait_send())

        @pl.when(jnp.logical_not(end))
        def _(h=h):
            z_copy(h, mirrored(2), mirrored(0), 1).wait_send()

        for t in range(Z):
            s_copy(h, t).wait_send()
            s2_copy(h, t).wait_send()

            @pl.when(z != t)
            def _(h=h, t=t):
                c_copy(h, t).wait_send()

        p_copy(h).wait_send()
        d_copy(h).wait_send()
    for copy in (wa_copy, ba_copy, wb_copy, bb_copy, we_copy, wf_copy):
        copy.wait_send()
    for off in range(1, Z):
        wc_copy(off).wait_send()
        bc_copy(off).wait_send()
        wd_copy(off).wait_send()


def fused_layer(adjacency, features, weights, bias_vector, cotangent, Z, FC):
    V, F = features.shape
    R, fc = 2 * Z, F // FC
    f32, bf16 = jnp.float32, jnp.bfloat16
    H, Q, P8 = F // 2, F // 4, F // (4 * Z)
    dma = pltpu.SemaphoreType.DMA
    vm = pltpu.VMEM
    scale = 1.0 / math.sqrt(V * R * 2)
    whole = pl.BlockSpec(memory_space=pltpu.VMEM)
    return pl.pallas_call(
        functools.partial(layer_kernel, Z, FC, scale),
        out_shape=(
            jax.ShapeDtypeStruct((V, F), bf16),
            jax.ShapeDtypeStruct((F, F), bf16),
            jax.ShapeDtypeStruct((1, F), f32),
            jax.ShapeDtypeStruct((V, F), bf16),
        ),
        in_specs=[pl.BlockSpec(memory_space=pl.ANY)] + [whole] * 4,
        out_specs=[whole] * 4,
        scratch_shapes=[
            vm((R, 2 * V, V), bf16), vm((FC, Z, 2, V, fc), bf16), vm((FC, 2 * V, fc), f32),
            vm((FC, V, fc), bf16), vm((FC, V, fc), bf16), vm((V, F), bf16), vm((V, F), bf16),
            vm((FC, 2, fc, V), bf16),
            vm((FC, Z, fc, V), bf16), vm((FC, Z, fc, V), bf16), vm((FC, Z, fc, V), bf16),
            vm((FC, Z, fc, V), bf16), vm((FC, Z, fc, V), bf16), vm((FC, fc, V), bf16),
            vm((fc, V), f32), vm((F, F), f32), vm((H, F), f32), vm((H, F), f32), vm((Q, F), bf16), vm((Q, F), bf16),
            vm((Z, P8, F), bf16), vm((Z, P8, F), bf16), vm((2, 2, Z, P8, F), bf16),
            vm((3, 8, F), f32), vm((2, 8, F), f32), vm((Z, 8, F), f32),
            dma((R,)), dma((FC, 2, Z)), dma((FC, Z)), dma((FC, Z)), dma((FC, Z)),
            dma((FC,)), dma((FC,)), dma((FC,)), dma((FC,)),
            dma((FC, Z)), dma((FC, Z)), dma((FC, Z)), dma((FC, Z)), dma((FC,)),
            dma((4,)), dma((4,)), dma((Z,)), dma((Z,)), dma((Z,)), dma((Z,)),
            dma((Z,)), dma((Z,)), dma((2,)), dma((2,)),
        ],
        compiler_params=pltpu.CompilerParams(
            collective_id=0, has_side_effects=True, vmem_limit_bytes=42 << 20
        ),
    )(adjacency, features, weights, bias_vector.reshape(1, F), cotangent)


def on_device_fused(
    features, weights, bias_vector, tile_values, tile_rows, tile_cols, tile_counts, cotangent
):
    tiles = tile_values[0, 0]
    rows = lax.axis_size("row")
    local_rows, edge = features.shape[0], tiles.shape[-1]
    adjacency = densify(
        tiles, tile_rows[0, 0], tile_cols[0, 0], tile_counts[0],
        local_rows * 2 // edge, local_rows * rows // edge, local_rows,
    )
    activated, weight_grad, bias_rows, feature_grad = fused_layer(
        adjacency, features, weights, bias_vector, cotangent, rows // 2, feature_chunks
    )
    return (activated, weight_grad.astype(jnp.float32), bias_rows[0], feature_grad)


def solution(mesh):
    in_specs = (
        P(("rep", "col", "row"), None),
        P(),
        P(),
        P(("rep", "row"), "col", None, None, None),
        P(("rep", "row"), "col", None),
        P(("rep", "row"), "col", None),
        P(("rep", "row"), "col"),
        P(("rep", "row", "col"), None),
    )
    out_specs = (
        P(("rep", "row", "col"), None),
        P("rep", None),
        P("rep"),
        P(("rep", "col", "row"), None),
    )
    small = mesh.shape["col"] == 2 and mesh.shape["row"] == 8
    return jax.shard_map(
        on_device_fused if small else on_device, mesh=mesh, in_specs=in_specs, out_specs=out_specs, check_vma=False
    )
```

```python
import functools
import math

import jax
import jax.numpy as jnp
from jax import lax
from jax.experimental import pallas as pl
from jax.experimental.pallas import tpu as pltpu
from jax.sharding import PartitionSpec as P

slot_group = 16
feature_chunks = 2


def tile_range(cols_in, live_count, first_block, last_block):
    slots = jnp.arange(cols_in.shape[0], dtype=jnp.int32)
    live = slots < live_count
    lower = jnp.sum((live & (cols_in < first_block)).astype(jnp.int32))
    upper = jnp.sum((live & (cols_in < last_block)).astype(jnp.int32))
    return (lower, upper)


def group_slots(tiles, rows_in, cols_in, begin, upper):
    limit = tiles.shape[0] - slot_group
    start = jnp.minimum(begin, limit)
    tile_group = lax.dynamic_slice_in_dim(tiles, start, slot_group, 0)
    row_group = lax.dynamic_slice_in_dim(rows_in, start, slot_group, 0)
    col_group = lax.dynamic_slice_in_dim(cols_in, start, slot_group, 0)
    slots = start + jnp.arange(slot_group, dtype=jnp.int32)
    live = ((slots >= begin) & (slots < upper)).astype(jnp.float32)
    return (tile_group, row_group, col_group, live)


def forward_tiles(carry, tiles, rows_in, cols_in, piece, first_block, lower, upper):
    edge = tiles.shape[-1]
    blocks = piece.reshape(-1, edge, piece.shape[-1])
    block_count = blocks.shape[0]
    group_total = (upper - lower + slot_group - 1) // slot_group

    def forward_step(group_index, accum):
        begin = lower + group_index * slot_group
        tile_group, row_group, col_group, live = group_slots(tiles, rows_in, cols_in, begin, upper)
        local = jnp.clip(col_group - first_block, 0, block_count - 1)
        taken = jnp.take(blocks, local, axis=0)
        product = jnp.einsum("gij,gjf->gif", tile_group, taken, preferred_element_type=jnp.float32)
        return accum.at[row_group].add(product * live[:, None, None])

    return lax.fori_loop(0, group_total, forward_step, carry)


def backward_tiles(carry, tiles, rows_in, cols_in, grad_blocks, first_block, lower, upper):
    block_count = carry.shape[0]
    group_total = (upper - lower + slot_group - 1) // slot_group

    def backward_step(group_index, accum):
        begin = lower + group_index * slot_group
        tile_group, row_group, col_group, live = group_slots(tiles, rows_in, cols_in, begin, upper)
        taken = jnp.take(grad_blocks, row_group, axis=0)
        product = jnp.einsum("gji,gjf->gif", tile_group, taken, preferred_element_type=jnp.float32)
        local = jnp.clip(col_group - first_block, 0, block_count - 1)
        return accum.at[local].add(product * live[:, None, None])

    return lax.fori_loop(0, group_total, backward_step, carry)


def on_device(
    features, weights, bias_vector, tile_values, tile_rows, tile_cols, tile_counts, cotangent
):
    tiles = tile_values[0, 0]
    rows_in = tile_rows[0, 0]
    cols_in = tile_cols[0, 0]
    live_count = tile_counts[0, 0]
    row_devs = lax.axis_size("row")
    col_devs = lax.axis_size("col")
    local_rows = features.shape[0]
    width = features.shape[1]
    edge = tiles.shape[-1]
    row_tiles = local_rows * col_devs // edge
    col_tiles = local_rows * row_devs // edge
    empty_rows = jnp.zeros((row_tiles, edge, width), jnp.float32)
    column_block = lax.all_gather(features, "row", axis=0, tiled=True)
    lower, upper = tile_range(cols_in, live_count, 0, col_tiles)
    partial_value = forward_tiles(
        empty_rows, tiles, rows_in, cols_in, column_block, 0, lower, upper
    )
    gathered = lax.psum_scatter(
        partial_value.reshape(row_tiles * edge, width).astype(jnp.bfloat16),
        "col",
        scatter_dimension=0,
        tiled=True,
    )
    pre = jnp.dot(gathered, weights, preferred_element_type=jnp.float32) + bias_vector
    sig = jax.nn.sigmoid(pre)
    activated = (pre * sig).astype(jnp.bfloat16)
    dpre = (cotangent.astype(jnp.float32) * sig * (1.0 + pre * (1.0 - sig))).astype(jnp.bfloat16)
    weight_local = lax.dot_general(
        gathered, dpre, (((0,), (0,)), ((), ())), preferred_element_type=jnp.float32
    )
    bias_local = jnp.sum(dpre.astype(jnp.float32), axis=0)
    weight_total, bias_total = lax.psum((weight_local, bias_local), ("row", "col"))
    scale = 1.0 / math.sqrt(local_rows * row_devs * col_devs)
    weight_grad = weight_total * scale
    bias_grad = bias_total * scale
    dgathered = lax.dot_general(
        dpre, weights, (((1,), (1,)), ((), ())), preferred_element_type=jnp.float32
    ).astype(jnp.bfloat16)
    row_block = lax.all_gather(dgathered, "col", axis=0, tiled=True)
    grad_blocks = row_block.reshape(row_tiles, edge, width)
    lower, upper = tile_range(cols_in, live_count, 0, col_tiles)
    empty_cols = jnp.zeros((col_tiles, edge, width), jnp.float32)
    term = backward_tiles(empty_cols, tiles, rows_in, cols_in, grad_blocks, 0, lower, upper)
    feature_sum = lax.psum_scatter(
        term.reshape(col_tiles * edge, width).astype(jnp.bfloat16),
        "row",
        scatter_dimension=0,
        tiled=True,
    )
    return (activated, weight_grad, bias_grad, feature_sum)


MESH = pl.DeviceIdType.MESH


def densify(tiles, rows_in, cols_in, live_count, row_tiles, col_tiles, wide):
    slots, edge = tiles.shape[0], tiles.shape[-1]
    per_step = wide // edge
    steps = col_tiles // per_step

    pieces = slots // slot_group

    def body(rows_ref, cols_ref, count_ref, tiles_hbm, out_ref, tiles_ref, accum, cursor, sems):
        step = pl.program_id(0)
        count = count_ref[0]

        def piece_copy(piece):
            window = pl.ds(piece * slot_group, slot_group)
            return pltpu.make_async_copy(tiles_hbm.at[window], tiles_ref.at[window], sems.at[piece])

        @pl.when(step == 0)
        def _():
            cursor[0] = 0
            for piece in range(pieces):

                @pl.when(piece * slot_group < count)
                def _(piece=piece):
                    piece_copy(piece).start()

        for part in range(per_step):
            column = step * per_step + part
            accum[...] = jnp.zeros_like(accum)

            def more(slot):
                return (slot < count) & (cols_ref[jnp.minimum(slot, slots - 1)] == column)

            def add(slot):
                @pl.when(slot % slot_group == 0)
                def _():
                    piece_copy(slot // slot_group).wait()

                window = pl.ds(pl.multiple_of(rows_ref[slot] * edge, edge), edge)
                accum[window, :] += tiles_ref[slot].astype(jnp.float32)
                return slot + 1

            cursor[0] = lax.while_loop(more, add, cursor[0])
            out_ref[0, :, part * edge : (part + 1) * edge] = accum[...].astype(jnp.bfloat16)

    return pl.pallas_call(
        body,
        out_shape=jax.ShapeDtypeStruct((steps, row_tiles * edge, wide), jnp.bfloat16),
        grid_spec=pltpu.PrefetchScalarGridSpec(
            num_scalar_prefetch=3,
            grid=(steps,),
            in_specs=[pl.BlockSpec(memory_space=pltpu.HBM)],
            out_specs=pl.BlockSpec((1, row_tiles * edge, wide), lambda s, *_: (s, 0, 0)),
            scratch_shapes=[
                pltpu.VMEM(tiles.shape, tiles.dtype),
                pltpu.VMEM((row_tiles * edge, edge), jnp.float32),
                pltpu.SMEM((1,), jnp.int32),
                pltpu.SemaphoreType.DMA((pieces,)),
            ],
        ),
        compiler_params=pltpu.CompilerParams(vmem_limit_bytes=12 << 20),
    )(rows_in, cols_in, live_count, tiles)


def layer_kernel(
    Z, FC, scale,
    a_hbm, x_ref, w_ref, b_ref, cot_ref,
    act_ref, wg_ref, bg_ref, fg_ref,
    av, xg, acc, psend, precv, gath, dpre_s, dg,
    own, sbuf, srecv, csend, crecv,
    fsum, wl, wra, wa, wab, wrb, wb, wrc, wfin, bs, br, br2,
    a_sem, gz_s, gz_r, gs_s, gs_r, p_s, p_r, d_s, d_r,
    s_s, s_r, c_s, c_r, w_s, w_r, wz_s, wz_r, wf_s, wf_r, bz_s, bz_r, bx_s, bx_r,
):
    r = lax.axis_index("row")
    c = lax.axis_index("col")
    z, k = r // 2, r % 2
    V, F = x_ref.shape
    fc = F // FC
    f32, bf16 = jnp.float32, jnp.bfloat16
    sib = {"row": z * 2 + (1 - k)}
    peer = {"col": 1 - c}

    def at_z(t):
        return {"row": t * 2 + k}

    def rc(src, dst, ss, rs, dev):
        return pltpu.make_async_remote_copy(
            src_ref=src, dst_ref=dst, send_sem=ss, recv_sem=rs, device_id=dev, device_id_type=MESH
        )

    def got(dst, rs):
        rc(dst, dst, d_s.at[0], rs, sib).wait_recv()

    for s in range(2 * Z):
        pltpu.make_async_copy(a_hbm.at[s], av.at[s], a_sem.at[s]).start()

    barrier = pltpu.get_barrier_semaphore()
    pl.semaphore_signal(barrier, inc=1, device_id=sib, device_id_type=MESH)
    pl.semaphore_signal(barrier, inc=1, device_id=peer, device_id_type=MESH)
    for off in range(1, Z):
        pl.semaphore_signal(barrier, inc=1, device_id=at_z((z + off) % Z), device_id_type=MESH)
    for h in range(FC):
        xg[h, z, k] = x_ref[:, h * fc : (h + 1) * fc]
    pl.semaphore_wait(barrier, Z + 1)

    end = (z == 0) | (z == Z - 1)

    def mirrored(position):
        return jnp.where(z * 2 < Z, position, Z - 1 - position)

    def z_copy(h, t, step):
        slot = xg.at[h, t, k]
        return rc(slot, slot, gz_s.at[h, (1 - step) // 2, t], gz_r.at[h, t], at_z(z + step))

    def s_copy(h, t):
        slot = xg.at[h, t, k]
        return rc(slot, slot, gs_s.at[h, t], gs_r.at[h, t], sib)

    def own_sends(h):
        @pl.when(z < Z - 1)
        def _():
            z_copy(h, z, 1).start()

        @pl.when(z > 0)
        def _():
            z_copy(h, z, -1).start()

        s_copy(h, z).start()

    def mm(h, t, plane, first=False):
        s = t * 2 + plane
        if h == 0:
            pltpu.make_async_copy(a_hbm.at[s], av.at[s], a_sem.at[s]).wait()
        prod = jnp.dot(av[s], xg[h, t, plane], preferred_element_type=f32)
        if first:
            acc[h] = prod
        else:
            acc[h] += prod

    def p_copy(h):
        return rc(psend.at[h], precv.at[h], p_s.at[h], p_r.at[h], peer)

    def share(h):
        psend[h] = acc[h, pl.ds(pl.multiple_of((1 - c) * V, V), V), :].astype(bf16)
        p_copy(h).start()

    for h in range(FC):
        own_sends(h)
    for h in range(FC):
        mm(h, z, k, True)
    for h in range(FC):
        got(xg.at[h, z, 1 - k], gs_r.at[h, z])
        mm(h, z, 1 - k)
    for dist in range(1, Z):
        for h in range(FC):
            sides = ((z - dist, z - dist >= 0, 1), (z + dist, z + dist < Z, -1))
            for t, valid, step in sides:

                @pl.when(valid)
                def _(h=h, t=t, step=step):
                    got(xg.at[h, t, k], gz_r.at[h, t])

                    @pl.when((z + step >= 0) & (z + step < Z))
                    def _():
                        z_copy(h, t, step).start()

                    s_copy(h, t).start()

            for t, valid, step in sides:

                @pl.when(valid)
                def _(h=h, t=t):
                    mm(h, t, k)
                    got(xg.at[h, t, 1 - k], gs_r.at[h, t])
                    mm(h, t, 1 - k)

            if dist == Z - 1:
                share(h)

    pre = jnp.broadcast_to(b_ref[...], (V, F))
    for h in range(FC):
        p_copy(h).wait_recv()
        g = acc[h, pl.ds(pl.multiple_of(c * V, V), V), :] + precv[h].astype(f32)
        gath[:, h * fc : (h + 1) * fc] = g.astype(bf16)
        pre = pre + jnp.dot(
            g.astype(bf16), w_ref[h * fc : (h + 1) * fc, :], preferred_element_type=f32
        )
    sig = jax.nn.sigmoid(pre)
    act_ref[...] = (pre * sig).astype(bf16)
    dval = (cot_ref[...].astype(f32) * sig * (1.0 + pre * (1.0 - sig))).astype(bf16)
    dpre_s[...] = dval

    def d_copy(h):
        slot = dg.at[h, c]
        return rc(slot, slot, d_s.at[h], d_r.at[h], peer)

    for h in range(FC):
        dg[h, c] = lax.dot_general(
            w_ref[h * fc : (h + 1) * fc, :], dpre_s[...], (((1,), (1,)), ((), ())),
            preferred_element_type=f32,
        ).astype(bf16)
        d_copy(h).start()

    bs[0] = jnp.sum(dpre_s[...].astype(f32).reshape(V // 8, 8, F), axis=0)
    wl[...] = lax.dot_general(
        gath[...], dpre_s[...], (((0,), (0,)), ((), ())), preferred_element_type=f32
    )
    H, Q, P8 = F // 2, F // 4, F // (4 * Z)
    wa_copy = rc(wl.at[pl.ds(pl.multiple_of((1 - k) * H, H), H), :], wra, w_s.at[0], w_r.at[0], sib)
    ba_copy = rc(bs.at[0], br.at[0], bx_s.at[0], bx_r.at[0], sib)
    wb_copy = rc(wab, wrb, w_s.at[1], w_r.at[1], peer)
    bb_copy = rc(bs.at[1], br.at[1], bx_s.at[1], bx_r.at[1], peer)
    we_copy = rc(wfin.at[k, c], wfin.at[k, c], w_s.at[2], w_r.at[2], peer)
    wf_copy = rc(wfin.at[k], wfin.at[k], w_s.at[3], w_r.at[3], sib)

    def wc_copy(off):
        t = (z + off) % Z
        return rc(wb.at[t], wrc.at[off], wz_s.at[off], wz_r.at[off], at_z(t))

    def wd_copy(off):
        t = (z + off) % Z
        return rc(wfin.at[k, c, z], wfin.at[k, c, z], wf_s.at[off], wf_r.at[off], at_z(t))

    def bc_copy(off):
        t = (z + off) % Z
        return rc(bs.at[2], br2.at[off], bz_s.at[off], bz_r.at[off], at_z(t))

    wa_copy.start()
    ba_copy.start()

    def stage_b():
        wa_copy.wait_recv()
        ba_copy.wait_recv()
        wa[...] = wl[pl.ds(pl.multiple_of(k * H, H), H), :] + wra[...]
        wab[...] = wa[pl.ds(pl.multiple_of((1 - c) * Q, Q), Q), :].astype(bf16)
        bs[1] = bs[0] + br[0]
        wb_copy.start()
        bb_copy.start()

    def stage_c():
        wb_copy.wait_recv()
        bb_copy.wait_recv()
        both = wa[pl.ds(pl.multiple_of(c * Q, Q), Q), :] + wrb[...].astype(f32)
        wb[...] = both.astype(bf16).reshape(Z, P8, F)
        bs[2] = bs[1] + br[1]
        for off in range(1, Z):
            wc_copy(off).start()
            bc_copy(off).start()

    def stage_d():
        total = wb[z].astype(f32)
        btotal = bs[2]
        for off in range(1, Z):
            wc_copy(off).wait_recv()
            bc_copy(off).wait_recv()
            total = total + wrc[off].astype(f32)
            btotal = btotal + br2[off]
        wfin[k, c, z] = (total * scale).astype(bf16)
        bg_ref[...] = jnp.sum(btotal, axis=0, keepdims=True) * scale
        for off in range(1, Z):
            wd_copy(off).start()

    def stage_e():
        for off in range(1, Z):
            t = (z - off + Z) % Z
            got(wfin.at[k, c, t], wf_r.at[off])
        we_copy.start()

    def stage_f():
        got(wfin.at[k, 1 - c], w_r.at[2])
        wf_copy.start()

    def s2_copy(h, d):
        return rc(sbuf.at[h, d], srecv.at[h, d], s_s.at[h, d], s_r.at[h, d], sib)

    def c_copy(h, d, step):
        place = jnp.where((step < 0) & (d == z - 1), Z, d)
        return rc(
            csend.at[h, d], crecv.at[h, place], c_s.at[h, d], c_r.at[h, place], at_z(z + step)
        )

    def bmm(h, d, plane):
        s = d * 2 + plane
        total = jnp.dot(dg[h, 0], av[s, :V, :], preferred_element_type=f32)
        total = total + jnp.dot(dg[h, 1], av[s, V:, :], preferred_element_type=f32)
        return total.astype(bf16)

    def target(i):
        return mirrored(jnp.where(end, Z - 1 - i, (i + 2) % Z))

    def local_sum(h, d):
        s2_copy(h, d).wait_recv()
        return own[h, d].astype(f32) + srecv[h, d].astype(f32)

    def products(i, carry):
        d = target(i)
        for h in range(FC):

            @pl.when(i == 0)
            def _(h=h):
                got(dg.at[h, 1 - c], d_r.at[h])

            sbuf[h, d] = bmm(h, d, 1 - k)
            s2_copy(h, d).start()
            own[h, d] = bmm(h, d, k)

            @pl.when(end & (i < Z - 1))
            def _(h=h):
                csend[h, d] = local_sum(h, d).astype(bf16)
                c_copy(h, d, jnp.where(z == 0, 1, -1)).start()

        return carry

    inward = jnp.where(z * 2 < Z, 1, -1)

    def forward(d, step):
        @pl.when(jnp.logical_not(end))
        def _():
            for h in range(FC):
                got(crecv.at[h, d], c_r.at[h, d])
                csend[h, d] = (local_sum(h, d) + crecv[h, d].astype(f32)).astype(bf16)
                c_copy(h, d, step).start()

    def finish(h):
        s2_copy(h, z).wait_recv()
        fsum[...] = own[h, z].astype(f32) + srecv[h, z].astype(f32)

        @pl.when(z > 0)
        def _():
            got(crecv.at[h, z], c_r.at[h, z])
            fsum[...] += crecv[h, z].astype(f32)

        @pl.when(z < Z - 1)
        def _():
            got(crecv.at[h, Z], c_r.at[h, Z])
            fsum[...] += crecv[h, Z].astype(f32)

        fg_ref[:, h * fc : (h + 1) * fc] = fsum[...].T.astype(bf16)

    lax.fori_loop(0, Z, products, 0)
    stage_b()
    forward(mirrored(3), inward)
    stage_c()
    forward(mirrored(0), -inward)
    forward(mirrored(2), inward)
    stage_d()
    for h in range(FC - 1):
        finish(h)
    stage_e()
    finish(FC - 1)
    stage_f()
    got(wfin.at[1 - k], w_r.at[3])
    wg_ref[...] = wfin[...].reshape(F, F)

    for h in range(FC):
        for t in range(Z):

            @pl.when((z < Z - 1) & (t <= z))
            def _(h=h, t=t):
                z_copy(h, t, 1).wait_send()

            @pl.when((z > 0) & (t >= z))
            def _(h=h, t=t):
                z_copy(h, t, -1).wait_send()

            s_copy(h, t).wait_send()
            s2_copy(h, t).wait_send()

            @pl.when(z != t)
            def _(h=h, t=t):
                c_copy(h, t, jnp.where(z < t, 1, -1)).wait_send()

        p_copy(h).wait_send()
        d_copy(h).wait_send()
    for copy in (wa_copy, ba_copy, wb_copy, bb_copy, we_copy, wf_copy):
        copy.wait_send()
    for off in range(1, Z):
        wc_copy(off).wait_send()
        bc_copy(off).wait_send()
        wd_copy(off).wait_send()


def fused_layer(adjacency, features, weights, bias_vector, cotangent, Z, FC):
    V, F = features.shape
    R, fc = 2 * Z, F // FC
    f32, bf16 = jnp.float32, jnp.bfloat16
    H, Q, P8 = F // 2, F // 4, F // (4 * Z)
    dma = pltpu.SemaphoreType.DMA
    vm = pltpu.VMEM
    scale = 1.0 / math.sqrt(V * R * 2)
    whole = pl.BlockSpec(memory_space=pltpu.VMEM)
    return pl.pallas_call(
        functools.partial(layer_kernel, Z, FC, scale),
        out_shape=(
            jax.ShapeDtypeStruct((V, F), bf16),
            jax.ShapeDtypeStruct((F, F), bf16),
            jax.ShapeDtypeStruct((1, F), f32),
            jax.ShapeDtypeStruct((V, F), bf16),
        ),
        in_specs=[pl.BlockSpec(memory_space=pl.ANY)] + [whole] * 4,
        out_specs=[whole] * 4,
        scratch_shapes=[
            vm((R, 2 * V, V), bf16), vm((FC, Z, 2, V, fc), bf16), vm((FC, 2 * V, fc), f32),
            vm((FC, V, fc), bf16), vm((FC, V, fc), bf16), vm((V, F), bf16), vm((V, F), bf16),
            vm((FC, 2, fc, V), bf16),
            vm((FC, Z, fc, V), bf16), vm((FC, Z, fc, V), bf16), vm((FC, Z, fc, V), bf16),
            vm((FC, Z, fc, V), bf16), vm((FC, Z + 1, fc, V), bf16),
            vm((fc, V), f32), vm((F, F), f32), vm((H, F), f32), vm((H, F), f32), vm((Q, F), bf16), vm((Q, F), bf16),
            vm((Z, P8, F), bf16), vm((Z, P8, F), bf16), vm((2, 2, Z, P8, F), bf16),
            vm((3, 8, F), f32), vm((2, 8, F), f32), vm((Z, 8, F), f32),
            dma((R,)), dma((FC, 2, Z)), dma((FC, Z)), dma((FC, Z)), dma((FC, Z)),
            dma((FC,)), dma((FC,)), dma((FC,)), dma((FC,)),
            dma((FC, Z)), dma((FC, Z)), dma((FC, Z)), dma((FC, Z + 1)),
            dma((4,)), dma((4,)), dma((Z,)), dma((Z,)), dma((Z,)), dma((Z,)),
            dma((Z,)), dma((Z,)), dma((2,)), dma((2,)),
        ],
        compiler_params=pltpu.CompilerParams(
            collective_id=0, has_side_effects=True, vmem_limit_bytes=42 << 20
        ),
    )(adjacency, features, weights, bias_vector.reshape(1, F), cotangent)


def on_device_fused(
    features, weights, bias_vector, tile_values, tile_rows, tile_cols, tile_counts, cotangent
):
    tiles = tile_values[0, 0]
    rows = lax.axis_size("row")
    local_rows, edge = features.shape[0], tiles.shape[-1]
    adjacency = densify(
        tiles, tile_rows[0, 0], tile_cols[0, 0], tile_counts[0],
        local_rows * 2 // edge, local_rows * rows // edge, local_rows,
    )
    activated, weight_grad, bias_rows, feature_grad = fused_layer(
        adjacency, features, weights, bias_vector, cotangent, rows // 2, feature_chunks
    )
    return (activated, weight_grad.astype(jnp.float32), bias_rows[0], feature_grad)


def solution(mesh):
    in_specs = (
        P(("rep", "col", "row"), None),
        P(),
        P(),
        P(("rep", "row"), "col", None, None, None),
        P(("rep", "row"), "col", None),
        P(("rep", "row"), "col", None),
        P(("rep", "row"), "col"),
        P(("rep", "row", "col"), None),
    )
    out_specs = (
        P(("rep", "row", "col"), None),
        P("rep", None),
        P("rep"),
        P(("rep", "col", "row"), None),
    )
    small = mesh.shape["col"] == 2 and mesh.shape["row"] == 8
    return jax.shard_map(
        on_device_fused if small else on_device, mesh=mesh, in_specs=in_specs, out_specs=out_specs, check_vma=False
    )
```
